32 devices in a mesh: dp: 16 (over z, y, core), own: 2 (over x).
Axes of the slice: x: 2, y: 2, z: 4, core: 2. Of those that a mesh axis runs over, the one named last changes fastest.
Arguments:
- layer_inputs: bfloat16 [4, 16, 16, 128, 128], P(None, 'dp', 'own'), as said below
- weights: bfloat16 [4, 1152, 128], replicated, may hold values from -0.1875 to 0.1875
- top_cotangent: bfloat16 [16, 16, 128, 128], P('dp', 'own'), may hold values from -6 to 6
- segmentation: int32 [16, 16, 128], P('dp', 'own'), may hold values from 0 to 2
- layer_slots: int32 [4], replicated, may hold values from 0 to 3, as said below
- a_inverse: bfloat16 [4, 1152, 1152], P('own', 'dp'), as said below
- g_inverse: bfloat16 [4, 128, 128], P('own'), as said below
Outputs:
- preconditioned: float32 [4, 1152, 128], P(None, 'dp')
- input_grad: bfloat16 [16, 16, 128, 128], P('dp', 'own')
The draws below stay inside these ranges and needn't reach their ends.
Inputs may be any that keep to these rules, and one draw needn't show every extreme that they name: Distinct slot numbers; layer l is held by owner layer_slots[l] // 2, in that owner's slot layer_slots[l] % 2. One owner holds exactly 2 layers in every draw. `a_inverse`: each factor is symmetric. `g_inverse`: each factor is symmetric. `layer_inputs`: activations after a rectifier.
All inputs are finite; a program needn't handle non-finite values.
Results may differ from the reference program's by a relative error of at most 0.011.
Values may be sent and summed in bfloat16 or wider, within the bound.
A program may use at most 64 MiB of HBM per device.

```python
import math
import jax
import jax.numpy as jnp
from jax import lax

C = 128
LAYERS = 4
SLOTS = 2
COLS = 128
OWNERS = 2
SLICES = 16
ROWS = 16
PIXELS = 32768


def symmetric_inverse(key, mat_count, mat_order, low_log, high_log):
    key_off, key_diag, key_scale = jax.random.split(key, 3)
    spread = jax.random.uniform(key_off, (mat_count, mat_order, mat_order), jnp.float32, -1.0, 1.0) * (1.5 / math.sqrt(mat_order))
    spread = 0.5 * (spread + jnp.swapaxes(spread, 1, 2))
    diagonal = jax.random.uniform(key_diag, (mat_count, mat_order), jnp.float32, 1.5, 2.5)
    factors = jnp.exp(jax.random.uniform(key_scale, (mat_count, mat_order), jnp.float32, low_log, high_log))
    identity = jnp.eye(mat_order, dtype=jnp.float32)
    matrix_core = spread * (1.0 - identity) + identity * diagonal[:, :, None]
    return matrix_core * factors[:, :, None] * factors[:, None, :]


def draw_a_inverse(key, part):
    return symmetric_inverse(jax.random.fold_in(key, 11), OWNERS * SLOTS, 9 * C, math.log(0.5), math.log(2.0)).astype(jnp.bfloat16)


def draw_g_inverse(key, part):
    return symmetric_inverse(jax.random.fold_in(key, 23), OWNERS * SLOTS, C, math.log(0.5), math.log(2.0)).astype(jnp.bfloat16)


def draw_layer_inputs(key, part):
    full_shape = (LAYERS, SLICES, ROWS, COLS, C)
    key_main = jax.random.fold_in(jax.random.fold_in(key, 37), 0)
    values = jax.random.normal(key_main, full_shape, jnp.float32)
    return jnp.maximum(values, 0.0).astype(jnp.bfloat16)


def draw_layer_slots(key, part):
    key_full, key_rest, key_order = jax.random.split(jax.random.fold_in(key, 51), 3)
    busiest = jax.random.randint(key_full, (), 0, OWNERS)
    others = jax.random.permutation(key_rest, (OWNERS - 1) * SLOTS)[:LAYERS - SLOTS]
    others = jnp.where(others >= busiest * SLOTS, others + SLOTS, others)
    filled = busiest * SLOTS + jnp.arange(SLOTS)
    chosen = jnp.concatenate([filled, others])
    shuffle = jax.random.permutation(key_order, LAYERS)
    return chosen[shuffle].astype(jnp.int32)


def set_ends(result, stream_key, smallest, top_value):
    place = [jax.random.randint(jax.random.fold_in(stream_key, axis), (), 0, length) for axis, length in enumerate(result.shape)]
    main_axis = result.shape.index(max(result.shape))
    next_to = place[:main_axis] + [(place[main_axis] + 1) % result.shape[main_axis]] + place[main_axis + 1:]
    return result.at[tuple(place)].set(smallest).at[tuple(next_to)].set(top_value)


def levels(rng, shape, cuts, smallest, largest):
    def one(dim, shards_of):
        heights = jax.random.uniform(jax.random.fold_in(jax.random.fold_in(rng, 6), dim), (shards_of,), jnp.float32, smallest / len(cuts), largest / len(cuts))
        return jnp.repeat(jnp.exp(heights), shape[dim] // shards_of).reshape((-1,) + (1,) * (len(shape) - dim - 1))

    loudness = one(*cuts[0])
    for cut in cuts[1:]:
        loudness = loudness * one(*cut)
    return loudness


def gaussian(stream_key, dims, deviation, reach, cuts=(), kind=jnp.bfloat16):
    result = deviation * jax.random.normal(stream_key, dims, jnp.float32)
    if cuts:
        result = result * levels(stream_key, dims, cuts, -0.22, 0.18)
    return jnp.clip(result, -reach, reach).astype(kind)


def setup_inputs(seed: int = 0) -> dict:
    key_list = jax.random.split(jax.random.key(seed), 8)
    return {
        "layer_inputs": draw_layer_inputs(jax.random.fold_in(key_list[7], 71), 0),
        "weights": gaussian(key_list[1], (LAYERS, 9 * C, C), (9 * C) ** -0.5, 0.1875),
        "top_cotangent": gaussian(key_list[2], (SLICES, ROWS, COLS, C), 1.0, 6.0, ((0, 16), (1, 2))),
        "segmentation": set_ends(jax.random.randint(key_list[3], (SLICES, ROWS, COLS), 0, 3), jax.random.fold_in(key_list[3], 1), 0, 2).astype(jnp.int32),
        "layer_slots": draw_layer_slots(jax.random.fold_in(key_list[7], 71), 0),
        "a_inverse": draw_a_inverse(jax.random.fold_in(key_list[7], 71), 0),
        "g_inverse": draw_g_inverse(jax.random.fold_in(key_list[7], 71), 0),
    }


def loss_weight(labels):
    return jnp.where(labels == 0, 1.0, jnp.where(labels == 1, 0.0, 0.5)).astype(jnp.float32)

def tap_matrix(padded, num_rows, num_cols):
    channels = padded.shape[-1]
    pieces = []
    for tap_index in range(9):
        row_start = 2 - tap_index // 3
        col_start = 2 - tap_index % 3
        pieces.append(padded[row_start:row_start + num_rows, col_start:col_start + num_cols])
    stacked = jnp.stack(pieces, axis=2)
    return stacked.reshape(num_rows * num_cols, 9 * channels)

def slice_pass(inputs_slice, cotangent_slice, labels_slice, weights):
    num_rows = cotangent_slice.shape[0]
    num_cols = cotangent_slice.shape[1]
    channels = cotangent_slice.shape[2]
    scaled = loss_weight(labels_slice)[:, :, None] * cotangent_slice.astype(jnp.float32)
    out_grad = scaled.astype(jnp.bfloat16)
    layer_grads = [None] * LAYERS
    first_grad = None
    for layer_index in range(LAYERS - 1, -1, -1):
        padded = jnp.pad(out_grad, ((1, 1), (1, 1), (0, 0)))
        tap_rows = tap_matrix(padded, num_rows, num_cols)
        flat_inputs = inputs_slice[layer_index].reshape(num_rows * num_cols, channels)
        layer_grads[layer_index] = lax.dot_general(flat_inputs, tap_rows, (((0,), (0,)), ((), ())), preferred_element_type=jnp.float32)
        kernel = weights[layer_index].reshape(channels, 9 * channels)
        input_side = lax.dot_general(tap_rows, kernel, (((1,), (1,)), ((), ())), preferred_element_type=jnp.float32)
        input_side = input_side.reshape(num_rows, num_cols, channels)
        if layer_index > 0:
            active = inputs_slice[layer_index] > 0
            out_grad = jnp.where(active, input_side, 0.0).astype(jnp.bfloat16)
        else:
            first_grad = input_side.astype(jnp.bfloat16)
    return (jnp.stack(layer_grads, axis=0), first_grad)

def reference(layer_inputs, weights, top_cotangent, segmentation, layer_slots, a_inverse, g_inverse):
    channels = weights.shape[-1]

    def accumulate(running, slice_index):
        inputs_slice = lax.dynamic_index_in_dim(layer_inputs, slice_index, 1, keepdims=False)
        cotangent_slice = lax.dynamic_index_in_dim(top_cotangent, slice_index, 0, keepdims=False)
        labels_slice = lax.dynamic_index_in_dim(segmentation, slice_index, 0, keepdims=False)
        layer_grads, first_grad = slice_pass(inputs_slice, cotangent_slice, labels_slice, weights)
        return (running + layer_grads, first_grad)
    start_total = jnp.zeros((LAYERS, channels, 9 * channels), jnp.float32)
    grad_total, input_grad = lax.scan(accumulate, start_total, jnp.arange(SLICES, dtype=jnp.int32))
    grad_half = (grad_total * (1.0 / math.sqrt(PIXELS))).astype(jnp.bfloat16)
    grad_half = grad_half.reshape(LAYERS, 9 * channels, channels)
    inverse_left = jnp.take(a_inverse, layer_slots, axis=0)
    inverse_right = jnp.take(g_inverse, layer_slots, axis=0)
    left_product = jnp.einsum('lij,ljc->lic', inverse_left.astype(jnp.float32), grad_half.astype(jnp.float32)).astype(jnp.bfloat16)
    preconditioned = jnp.einsum('lic,lcd->lid', left_product.astype(jnp.float32), inverse_right.astype(jnp.float32))
    return (preconditioned, input_grad)
```

```python
import functools
import math

import jax
import jax.numpy as jnp
from jax import lax
from jax.experimental import pallas as pl
from jax.experimental.pallas import tpu as pltpu
from jax.sharding import PartitionSpec as P


def extended(cells, sides, width):
    for axis, dim in sides:
        count = lax.axis_size(axis)
        ends = count - 1
        head = lax.slice_in_dim(cells, 0, width, axis=dim)
        tail = lax.slice_in_dim(cells, cells.shape[dim] - width, cells.shape[dim], axis=dim)
        cells = jnp.concatenate(
            [
                lax.ppermute(tail, axis, [(i, (i + 1) % count) for i in range(ends)]),
                cells,
                lax.ppermute(head, axis, [((i + 1) % count, i) for i in range(ends)]),
            ],
            axis=dim,
        )
    return cells


def from_root(block, axis, owner):
    block = jnp.where(lax.axis_index(axis) == owner, block, jnp.zeros_like(block))
    return lax.psum(block, axis)


def loss_weight(labels):
    return jnp.where(labels == 0, 1.0, jnp.where(labels == 1, 0.0, 0.5)).astype(jnp.float32)


def tap_matrix(padded, num_rows, num_cols):
    channels = padded.shape[-1]
    pieces = []
    for tap_index in range(9):
        row_start = 2 - tap_index // 3
        col_start = 2 - tap_index % 3
        pieces.append(padded[row_start : row_start + num_rows, col_start : col_start + num_cols])
    stacked = jnp.stack(pieces, axis=2)
    return stacked.reshape(num_rows * num_cols, 9 * channels)


def per_device(
    layer_inputs, weights, top_cotangent, segmentation, layer_slots, a_inverse, g_inverse
):
    layer_count = layer_inputs.shape[0]
    num_rows = layer_inputs.shape[2]
    num_cols = layer_inputs.shape[3]
    channels = layer_inputs.shape[4]
    data_devices = lax.axis_size("dp")
    owner_devices = lax.axis_size("own")
    grad_scale = 1.0 / math.sqrt(data_devices * owner_devices * num_rows * num_cols)
    inputs_local = layer_inputs[:, 0]
    scaled = loss_weight(segmentation[0])[:, :, None] * top_cotangent[0].astype(jnp.float32)
    out_grad = scaled.astype(jnp.bfloat16)
    grad_blocks = [None] * layer_count
    input_grad = None
    for layer_index in range(layer_count - 1, -1, -1):
        rimmed = extended(out_grad, (("own", 0),), 1)
        padded = jnp.pad(rimmed, ((0, 0), (1, 1), (0, 0)))
        tap_rows = tap_matrix(padded, num_rows, num_cols)
        flat_inputs = inputs_local[layer_index].reshape(num_rows * num_cols, channels)
        grad_block = lax.dot_general(
            flat_inputs, tap_rows, (((0,), (0,)), ((), ())), preferred_element_type=jnp.float32
        )
        grad_blocks[layer_index] = grad_block.reshape(9 * channels, channels) * grad_scale
        kernel = weights[layer_index].reshape(channels, 9 * channels)
        input_side = lax.dot_general(
            tap_rows, kernel, (((1,), (1,)), ((), ())), preferred_element_type=jnp.float32
        )
        input_side = input_side.reshape(num_rows, num_cols, channels)
        if layer_index > 0:
            out_grad = jnp.where(inputs_local[layer_index] > 0, input_side, 0.0).astype(
                jnp.bfloat16
            )
        else:
            input_grad = input_side.astype(jnp.bfloat16)[None]
    grad_term = jnp.concatenate(grad_blocks, axis=1)
    grad_rows = lax.psum_scatter(grad_term, "dp", scatter_dimension=0, tiled=True)
    slot_count = a_inverse.shape[0]
    grad_sum = lax.psum(grad_rows.astype(jnp.bfloat16), "own")
    left_panels = []
    right_panels = []
    for layer_index in range(layer_count):
        slot_id = layer_slots[layer_index]
        owner_index = slot_id // slot_count
        local_slot = slot_id % slot_count
        left_panel = lax.dynamic_index_in_dim(a_inverse, local_slot, 0, keepdims=False)
        right_panel = lax.dynamic_index_in_dim(g_inverse, local_slot, 0, keepdims=False)
        left_panel, right_panel = (
            from_root(left_panel, "own", owner_index),
            from_root(right_panel, "own", owner_index),
        )
        left_panels.append(left_panel)
        right_panels.append(right_panel)
    left_stack = jnp.stack(left_panels, axis=0)
    right_stack = jnp.stack(right_panels, axis=0)
    gathered_piece = lax.all_gather(grad_sum, "dp", axis=0, tiled=True)
    width_here = gathered_piece.shape[0]
    shaped_piece = gathered_piece.reshape(width_here, layer_count, channels)
    left_product = jnp.einsum(
        "lrn,nlc->lrc", left_stack, shaped_piece, preferred_element_type=jnp.float32
    )
    preconditioned = jnp.einsum(
        "lrc,lcd->lrd",
        left_product.astype(jnp.bfloat16),
        right_stack,
        preferred_element_type=jnp.float32,
    )
    return (preconditioned, input_grad)


BF = jnp.bfloat16
F32 = jnp.float32
MESH = pl.DeviceIdType.MESH


def whole_step_kernel(
    depth_count, reducers, grad_scale,
    slots_ref, x_ref, w_ref, cot_ref, seg_ref, a_ref, gi_ref,
    pre_ref, ig_ref,
    taps, w32, wt, grad32, sent, r1, half, r2, quart, r3, full,
    edge, halo, a_all, g_all,
    halo_s, halo_r, ex_s, ex_r, s1, t1, s2, t2, s3, t3, s4, t4, s5, t5, s6, t6,
):
    layer_count, num_rows, num_cols, channels = x_ref.shape
    pixels = num_rows * num_cols
    dp = lax.axis_index("dp")
    own = lax.axis_index("own")
    core = lax.rem(dp, 2)
    y = lax.rem(dp // 2, 2)
    z = dp // 4
    quarter = y * 2 + own
    slot_count = a_ref.shape[0]

    def core_peer():
        return (dp + 1 - 2 * core, own)

    def plane_peer(j):
        other_y = y if j < 2 else 1 - y
        other_own = own if j % 2 == 0 else 1 - own
        return ((z * 2 + other_y) * 2 + core, other_own)

    def plane_quarter(j):
        other_y = y if j < 2 else 1 - y
        other_own = own if j % 2 == 0 else 1 - own
        return other_y * 2 + other_own

    def depth_index(j):
        return lax.rem(z + j, depth_count)

    def depth_peer(j):
        return ((depth_index(j) * 2 + y) * 2 + core, own)

    def remote(src, dst, send_sem, recv_sem, device):
        return pltpu.make_async_remote_copy(
            src_ref=src, dst_ref=dst, send_sem=send_sem, recv_sem=recv_sem,
            device_id=device, device_id_type=MESH,
        )

    barrier = pltpu.get_barrier_semaphore()
    peers = [core_peer()] + [plane_peer(j) for j in range(1, 4)]
    peers += [depth_peer(j) for j in range(1, depth_count)]
    for peer in peers:
        pl.semaphore_signal(barrier, inc=1, device_id=peer, device_id_type=MESH)

    col_index = lax.broadcasted_iota(jnp.int32, (pixels, channels), 0) % num_cols

    def column_shifts(flat):
        count = flat.shape[0]
        index = col_index[:count]
        before = jnp.where(index == num_cols - 1, 0.0, pltpu.roll(flat, count - 1, 0))
        after = jnp.where(index == 0, 0.0, pltpu.roll(flat, 1, 0))
        return (before.astype(BF), flat.astype(BF), after.astype(BF))

    def build_taps(buf, grad):
        flat = grad.astype(F32)
        for b, piece in enumerate(column_shifts(flat)):
            taps[buf, 1 : num_rows + 1, :, b * channels : (b + 1) * channels] = piece.reshape(
                num_rows, num_cols, channels
            )

    halo_row = (num_rows + 1) * (1 - own)
    edge_row = (num_rows - 1) * (1 - own)

    def halo_copy(l):
        return remote(edge.at[l], halo.at[l], halo_s.at[l], halo_r.at[l], (dp, 1 - own))

    def a_copy():
        place = pl.ds(own * slot_count, slot_count)
        return remote(a_ref, a_all.at[place], ex_s.at[0], ex_r.at[0], (dp, 1 - own))

    def g_copy():
        place = pl.ds(own * slot_count, slot_count)
        return remote(gi_ref, g_all.at[place], ex_s.at[1], ex_r.at[1], (dp, 1 - own))

    def build_weights(l):
        w32[...] = w_ref[l].astype(F32)
        for k in range(9):
            wt[l, :, k * channels : (k + 1) * channels] = w32[
                pl.ds(k, channels, stride=9), :
            ].astype(BF)

    last = layer_count - 1
    labels = seg_ref[...]
    pixel_weight = jnp.where(labels == 0, 1.0, jnp.where(labels == 1, 0.0, 0.5)).astype(F32)
    by_column = pixel_weight.T
    rows = []
    for r in range(num_rows):
        rows.append((by_column[:, r : r + 1] * cot_ref[r].astype(F32)).astype(BF))
    for r in range(num_rows):
        ig_ref[r] = rows[r]
    edge[last] = ig_ref[edge_row]
    pl.semaphore_wait(barrier, len(peers))
    halo_copy(last).start()
    a_copy().start()
    g_copy().start()
    zero_row = jnp.zeros((num_cols, 3 * channels), BF)
    for buf in range(2):
        taps[buf, 0] = zero_row
        taps[buf, num_rows + 1] = zero_row
    build_taps(last % 2, ig_ref[...].reshape(pixels, channels))
    a_all[pl.ds(own * slot_count, slot_count)] = a_ref[...]
    g_all[pl.ds(own * slot_count, slot_count)] = gi_ref[...]

    def core_copy(l):
        return remote(sent.at[l, 1 - core], r1.at[l], s1.at[l], t1.at[l], core_peer())

    def plane_copy(l, j):
        return remote(
            half.at[l, plane_quarter(j)], r2.at[l, j - 1], s2.at[l, j - 1], t2.at[l, j - 1],
            plane_peer(j),
        )

    def depth_copy(l, j):
        return remote(
            quart.at[l, lax.min(depth_index(j), reducers - 1)], r3.at[l, j - 1],
            s3.at[l, j - 1], t3.at[l, j - 1], depth_peer(j),
        )

    def chunk_at(depth):
        return (core * 4 + quarter) * reducers + lax.min(depth, reducers - 1)

    def depth_back(l, j, place):
        return remote(full.at[l, place], full.at[l, place], s4.at[l, j - 1], t4.at[l, j - 1],
                      depth_peer(j))

    def plane_back(l, j, from_quarter):
        place = pl.ds((core * 4 + from_quarter) * reducers, reducers)
        return remote(full.at[l, place], full.at[l, place], s5.at[l, j - 1], t5.at[l, j - 1],
                      plane_peer(j))

    def core_back(l, from_core):
        place = pl.ds(from_core * 4 * reducers, 4 * reducers)
        return remote(full.at[l, place], full.at[l, place], s6.at[l], t6.at[l], core_peer())

    def stage_b(l):
        core_copy(l).wait()
        total = sent[l, core].astype(F32) + r1[l].astype(F32)
        half[l] = total.astype(BF).reshape(half.shape[1:])
        for j in range(1, 4):
            plane_copy(l, j).start()

    def stage_c(l):
        for j in range(1, 4):
            plane_copy(l, j).wait()
        total = half[l, quarter].astype(F32)
        for j in range(3):
            total = total + r2[l, j].astype(F32)
        quart[l] = total.astype(BF).reshape(quart.shape[1:])
        for j in range(1, depth_count):
            @pl.when(depth_index(j) < reducers)
            def _():
                depth_copy(l, j).start()

    def stage_d(l):
        for j in range(1, depth_count):
            @pl.when(depth_index(j) < reducers)
            def _():
                depth_copy(l, j).wait_send()

        @pl.when(z < reducers)
        def _():
            for j in range(1, depth_count):
                depth_copy(l, j).wait_recv()
            total = quart[l, lax.min(z, reducers - 1)].astype(F32)
            for j in range(depth_count - 1):
                total = total + r3[l, j].astype(F32)
            full[l, chunk_at(z)] = (total * grad_scale).astype(BF)
            for j in range(1, depth_count):
                depth_back(l, j, chunk_at(z)).start()

    def stage_e(l):
        for j in range(1, depth_count):
            source = depth_index(depth_count - j)

            @pl.when(source < reducers)
            def _():
                depth_back(l, j, chunk_at(source)).wait_recv()

        @pl.when(z < reducers)
        def _():
            for j in range(1, depth_count):
                depth_back(l, j, chunk_at(z)).wait_send()
        for j in range(1, 4):
            plane_back(l, j, quarter).start()

    def stage_f(l):
        for j in range(1, 4):
            plane_back(l, j, plane_quarter(j)).wait_recv()
            plane_back(l, j, quarter).wait_send()
        core_back(l, core).start()

    def stage_h(l):
        core_back(l, 1 - core).wait_recv()
        core_back(l, core).wait_send()
        slot = slots_ref[l]
        grad_half = full[l].reshape(9 * channels, channels)
        left = jnp.dot(a_all[slot], grad_half, preferred_element_type=F32)
        pre_ref[l] = jnp.dot(left.astype(BF), g_all[slot], preferred_element_type=F32)

    stages = [stage_b, stage_c, stage_d, stage_e, stage_f, stage_h]
    done = {l: 0 for l in range(layer_count)}

    def advance(ready):
        for l in range(layer_count - 1, ready - 1, -1):
            if done[l] < len(stages):
                if stages[done[l]] is stage_h and l == layer_count - 1:
                    a_copy().wait()
                    g_copy().wait()
                stages[done[l]](l)
                done[l] += 1

    contract_last = (((1,), (1,)), ((), ()))
    contract_first = (((0,), (0,)), ((), ()))
    for l in range(layer_count - 1, -1, -1):
        buf = l % 2
        build_weights(l)
        halo_copy(l).wait()
        for b, piece in enumerate(column_shifts(halo[l].astype(F32))):
            taps[buf, halo_row, :, b * channels : (b + 1) * channels] = piece
        if l > 0:
            side = jnp.zeros((num_cols, channels), F32)
            for a in range(3):
                side += lax.dot_general(
                    taps[buf, edge_row + 2 - a],
                    wt[l, :, a * 3 * channels : (a + 1) * 3 * channels],
                    contract_last, preferred_element_type=F32,
                )
            edge[l - 1] = jnp.where(x_ref[l, edge_row].astype(F32) > 0, side, 0.0).astype(BF)
            halo_copy(l - 1).start()
        side = jnp.zeros((pixels, channels), F32)
        for a in range(3):
            side += lax.dot_general(
                taps[buf, 2 - a : 2 - a + num_rows].reshape(pixels, 3 * channels),
                wt[l, :, a * 3 * channels : (a + 1) * 3 * channels],
                contract_last, preferred_element_type=F32,
            )
        if l > 0:
            active = x_ref[l].reshape(pixels, channels).astype(F32) > 0
            build_taps(1 - buf, jnp.where(active, side, 0.0).astype(BF))
        else:
            ig_ref[...] = side.astype(BF).reshape(num_rows, num_cols, channels)
        if l < last:
            advance(l + 1)
        flat_inputs = x_ref[l].reshape(pixels, channels)
        for a in range(3):
            block = lax.dot_general(
                flat_inputs,
                taps[buf, 2 - a : 2 - a + num_rows].reshape(pixels, 3 * channels),
                contract_first, preferred_element_type=F32,
            )
            for b in range(3):
                grad32[pl.ds(3 * a + b, channels, stride=9), :] = block[
                    :, b * channels : (b + 1) * channels
                ]
        sent[l] = grad32[...].astype(BF).reshape(sent.shape[1:])
        core_copy(l).start()
        if l < last:
            advance(l + 1)
    while done[0] < len(stages):
        advance(0)


def reducer_count(quarter_rows, depth_count):
    for count in range(depth_count, 0, -1):
        if quarter_rows % (16 * count) == 0:
            return count
    return 0


def fused_per_device(
    layer_inputs, weights, top_cotangent, segmentation, layer_slots, a_inverse, g_inverse
):
    layer_count = layer_inputs.shape[0]
    num_rows, num_cols, channels = layer_inputs.shape[2:]
    taps_rows = 9 * channels
    data_devices = lax.axis_size("dp")
    owner_devices = lax.axis_size("own")
    grad_scale = 1.0 / math.sqrt(data_devices * owner_devices * num_rows * num_cols)
    depth_count = data_devices // 4
    quarter_rows = taps_rows // 8
    reducers = reducer_count(quarter_rows, depth_count)
    chunk = quarter_rows // reducers
    slots_total = a_inverse.shape[0] * owner_devices
    n = layer_count
    vmem = pl.BlockSpec(memory_space=pltpu.VMEM)
    dma = pltpu.SemaphoreType.DMA
    return pl.pallas_call(
        functools.partial(whole_step_kernel, depth_count, reducers, grad_scale),
        out_shape=(
            jax.ShapeDtypeStruct((n, a_inverse.shape[1], channels), F32),
            jax.ShapeDtypeStruct((num_rows, num_cols, channels), BF),
        ),
        in_specs=[pl.BlockSpec(memory_space=pltpu.SMEM)] + [vmem] * 6,
        out_specs=(vmem, vmem),
        scratch_shapes=[
            pltpu.VMEM((2, num_rows + 2, num_cols, 3 * channels), BF),
            pltpu.VMEM((taps_rows, channels), F32),
            pltpu.VMEM((n, channels, taps_rows), BF),
            pltpu.VMEM((taps_rows, channels), F32),
            pltpu.VMEM((n, 2, taps_rows // 2, channels), BF),
            pltpu.VMEM((n, taps_rows // 2, channels), BF),
            pltpu.VMEM((n, 4, quarter_rows, channels), BF),
            pltpu.VMEM((n, 3, quarter_rows, channels), BF),
            pltpu.VMEM((n, reducers, chunk, channels), BF),
            pltpu.VMEM((n, depth_count - 1, chunk, channels), BF),
            pltpu.VMEM((n, 8 * reducers, chunk, channels), BF),
            pltpu.VMEM((n, num_cols, channels), BF),
            pltpu.VMEM((n, num_cols, channels), BF),
            pltpu.VMEM((slots_total,) + a_inverse.shape[1:], BF),
            pltpu.VMEM((slots_total,) + g_inverse.shape[1:], BF),
            dma((n,)), dma((n,)), dma((2,)), dma((2,)),
            dma((n,)), dma((n,)), dma((n, 3)), dma((n, 3)),
            dma((n, depth_count - 1)), dma((n, depth_count - 1)),
            dma((n, depth_count - 1)), dma((n, depth_count - 1)),
            dma((n, 3)), dma((n, 3)), dma((n,)), dma((n,)),
        ],
        compiler_params=pltpu.CompilerParams(
            collective_id=0, has_side_effects=True, vmem_limit_bytes=48 * 1024 * 1024
        ),
        name="whole_step",
    )(
        layer_slots, layer_inputs[:, 0], weights, top_cotangent[0], segmentation[0],
        a_inverse, g_inverse,
    )


def fused_step(*args):
    preconditioned, input_grad = fused_per_device(*args)
    return (preconditioned, input_grad[None])


def solution(mesh):
    in_specs = (
        P(None, "dp", "own", None, None),
        P(),
        P("dp", "own", None, None),
        P("dp", "own", None),
        P(),
        P("own", "dp", None),
        P("own", None, None),
    )
    out_specs = (P(None, "dp", None), P("dp", "own", None, None))
    fits = mesh.shape["own"] == 2 and mesh.shape["dp"] == 16
    return jax.shard_map(
        fused_step if fits else per_device,
        mesh=mesh, in_specs=in_specs, out_specs=out_specs, check_vma=False,
    )
```

```python
import functools
import math

import jax
import jax.numpy as jnp
from jax import lax
from jax.experimental import pallas as pl
from jax.experimental.pallas import tpu as pltpu
from jax.sharding import PartitionSpec as P


def extended(cells, sides, width):
    for axis, dim in sides:
        count = lax.axis_size(axis)
        ends = count - 1
        head = lax.slice_in_dim(cells, 0, width, axis=dim)
        tail = lax.slice_in_dim(cells, cells.shape[dim] - width, cells.shape[dim], axis=dim)
        cells = jnp.concatenate(
            [
                lax.ppermute(tail, axis, [(i, (i + 1) % count) for i in range(ends)]),
                cells,
                lax.ppermute(head, axis, [((i + 1) % count, i) for i in range(ends)]),
            ],
            axis=dim,
        )
    return cells


def from_root(block, axis, owner):
    block = jnp.where(lax.axis_index(axis) == owner, block, jnp.zeros_like(block))
    return lax.psum(block, axis)


def loss_weight(labels):
    return jnp.where(labels == 0, 1.0, jnp.where(labels == 1, 0.0, 0.5)).astype(jnp.float32)


def tap_matrix(padded, num_rows, num_cols):
    channels = padded.shape[-1]
    pieces = []
    for tap_index in range(9):
        row_start = 2 - tap_index // 3
        col_start = 2 - tap_index % 3
        pieces.append(padded[row_start : row_start + num_rows, col_start : col_start + num_cols])
    stacked = jnp.stack(pieces, axis=2)
    return stacked.reshape(num_rows * num_cols, 9 * channels)


def per_device(
    layer_inputs, weights, top_cotangent, segmentation, layer_slots, a_inverse, g_inverse
):
    layer_count = layer_inputs.shape[0]
    num_rows = layer_inputs.shape[2]
    num_cols = layer_inputs.shape[3]
    channels = layer_inputs.shape[4]
    data_devices = lax.axis_size("dp")
    owner_devices = lax.axis_size("own")
    grad_scale = 1.0 / math.sqrt(data_devices * owner_devices * num_rows * num_cols)
    inputs_local = layer_inputs[:, 0]
    scaled = loss_weight(segmentation[0])[:, :, None] * top_cotangent[0].astype(jnp.float32)
    out_grad = scaled.astype(jnp.bfloat16)
    grad_blocks = [None] * layer_count
    input_grad = None
    for layer_index in range(layer_count - 1, -1, -1):
        rimmed = extended(out_grad, (("own", 0),), 1)
        padded = jnp.pad(rimmed, ((0, 0), (1, 1), (0, 0)))
        tap_rows = tap_matrix(padded, num_rows, num_cols)
        flat_inputs = inputs_local[layer_index].reshape(num_rows * num_cols, channels)
        grad_block = lax.dot_general(
            flat_inputs, tap_rows, (((0,), (0,)), ((), ())), preferred_element_type=jnp.float32
        )
        grad_blocks[layer_index] = grad_block.reshape(9 * channels, channels) * grad_scale
        kernel = weights[layer_index].reshape(channels, 9 * channels)
        input_side = lax.dot_general(
            tap_rows, kernel, (((1,), (1,)), ((), ())), preferred_element_type=jnp.float32
        )
        input_side = input_side.reshape(num_rows, num_cols, channels)
        if layer_index > 0:
            out_grad = jnp.where(inputs_local[layer_index] > 0, input_side, 0.0).astype(
                jnp.bfloat16
            )
        else:
            input_grad = input_side.astype(jnp.bfloat16)[None]
    grad_term = jnp.concatenate(grad_blocks, axis=1)
    grad_rows = lax.psum_scatter(grad_term, "dp", scatter_dimension=0, tiled=True)
    slot_count = a_inverse.shape[0]
    grad_sum = lax.psum(grad_rows.astype(jnp.bfloat16), "own")
    left_panels = []
    right_panels = []
    for layer_index in range(layer_count):
        slot_id = layer_slots[layer_index]
        owner_index = slot_id // slot_count
        local_slot = slot_id % slot_count
        left_panel = lax.dynamic_index_in_dim(a_inverse, local_slot, 0, keepdims=False)
        right_panel = lax.dynamic_index_in_dim(g_inverse, local_slot, 0, keepdims=False)
        left_panel, right_panel = (
            from_root(left_panel, "own", owner_index),
            from_root(right_panel, "own", owner_index),
        )
        left_panels.append(left_panel)
        right_panels.append(right_panel)
    left_stack = jnp.stack(left_panels, axis=0)
    right_stack = jnp.stack(right_panels, axis=0)
    gathered_piece = lax.all_gather(grad_sum, "dp", axis=0, tiled=True)
    width_here = gathered_piece.shape[0]
    shaped_piece = gathered_piece.reshape(width_here, layer_count, channels)
    left_product = jnp.einsum(
        "lrn,nlc->lrc", left_stack, shaped_piece, preferred_element_type=jnp.float32
    )
    preconditioned = jnp.einsum(
        "lrc,lcd->lrd",
        left_product.astype(jnp.bfloat16),
        right_stack,
        preferred_element_type=jnp.float32,
    )
    return (preconditioned, input_grad)


BF = jnp.bfloat16
F32 = jnp.float32
MESH = pl.DeviceIdType.MESH


def whole_step_kernel(
    depth_count, reducers, grad_scale,
    slots_ref, x_hbm, w_hbm, cot_hbm, seg_hbm, a_hbm, gi_hbm,
    pre_ref, ig_ref,
    taps, w32, wt, grad32, sent, r1, half, r2, quart, r3, full,
    edge, halo, a_all, g_all, x_ref, w_ref, cot_ref, seg_ref, load,
    halo_s, halo_r, ex_s, ex_r, s1, t1, s2, t2, s3, t3, s4, t4, s5, t5, s6, t6,
):
    layer_count, num_rows, num_cols, channels = x_ref.shape
    pixels = num_rows * num_cols
    dp = lax.axis_index("dp")
    own = lax.axis_index("own")
    core = lax.rem(dp, 2)
    y = lax.rem(dp // 2, 2)
    z = dp // 4
    quarter = y * 2 + own
    slot_count = a_hbm.shape[0]
    held = pl.ds(own * slot_count, slot_count)

    def core_peer():
        return (dp + 1 - 2 * core, own)

    def plane_peer(j):
        other_y = y if j < 2 else 1 - y
        other_own = own if j % 2 == 0 else 1 - own
        return ((z * 2 + other_y) * 2 + core, other_own)

    def plane_quarter(j):
        other_y = y if j < 2 else 1 - y
        other_own = own if j % 2 == 0 else 1 - own
        return other_y * 2 + other_own

    def depth_index(j):
        return lax.rem(z + j, depth_count)

    def depth_peer(j):
        return ((depth_index(j) * 2 + y) * 2 + core, own)

    def remote(src, dst, send_sem, recv_sem, device):
        return pltpu.make_async_remote_copy(
            src_ref=src, dst_ref=dst, send_sem=send_sem, recv_sem=recv_sem,
            device_id=device, device_id_type=MESH,
        )

    last = layer_count - 1
    cot_load = pltpu.make_async_copy(cot_hbm, cot_ref, load.at[0])
    seg_load = pltpu.make_async_copy(seg_hbm, seg_ref, load.at[1])
    a_load = pltpu.make_async_copy(a_hbm, a_all.at[held], load.at[2])
    g_load = pltpu.make_async_copy(gi_hbm, g_all.at[held], load.at[3])

    def x_load(l):
        return pltpu.make_async_copy(x_hbm.at[l], x_ref.at[l], load.at[4 + l])

    def w_load(l):
        return pltpu.make_async_copy(w_hbm.at[l], w_ref.at[l], load.at[4 + layer_count + l])

    seg_load.start()
    cot_load.start()
    w_load(last).start()
    x_load(last).start()
    a_load.start()
    g_load.start()
    for l in range(last - 1, -1, -1):
        w_load(l).start()
        x_load(l).start()

    barrier = pltpu.get_barrier_semaphore()
    peers = [core_peer()] + [plane_peer(j) for j in range(1, 4)]
    peers += [depth_peer(j) for j in range(1, depth_count)]
    for peer in peers:
        pl.semaphore_signal(barrier, inc=1, device_id=peer, device_id_type=MESH)

    col_index = lax.broadcasted_iota(jnp.int32, (pixels, channels), 0) % num_cols

    def column_shifts(flat):
        count = flat.shape[0]
        index = col_index[:count]
        before = jnp.where(index == num_cols - 1, 0.0, pltpu.roll(flat, count - 1, 0))
        after = jnp.where(index == 0, 0.0, pltpu.roll(flat, 1, 0))
        return (before.astype(BF), flat.astype(BF), after.astype(BF))

    def build_taps(buf, grad):
        flat = grad.astype(F32)
        for b, piece in enumerate(column_shifts(flat)):
            taps[buf, 1 : num_rows + 1, :, b * channels : (b + 1) * channels] = piece.reshape(
                num_rows, num_cols, channels
            )

    halo_row = (num_rows + 1) * (1 - own)
    edge_row = (num_rows - 1) * (1 - own)

    def halo_copy(l):
        return remote(edge.at[l], halo.at[l], halo_s.at[l], halo_r.at[l], (dp, 1 - own))

    def a_copy(k):
        place = a_all.at[own * slot_count + k]
        return remote(place, place, ex_s.at[k], ex_r.at[k], (dp, 1 - own))

    def g_copy():
        return remote(g_all.at[held], g_all.at[held], ex_s.at[slot_count], ex_r.at[slot_count],
                      (dp, 1 - own))

    def factor_copies():
        return [a_copy(k) for k in range(slot_count)] + [g_copy()]

    def build_weights(l):
        w32[...] = w_ref[l].astype(F32)
        for k in range(9):
            wt[l, :, k * channels : (k + 1) * channels] = w32[
                pl.ds(k, channels, stride=9), :
            ].astype(BF)

    seg_load.wait()
    cot_load.wait()
    labels = seg_ref[...]
    pixel_weight = jnp.where(labels == 0, 1.0, jnp.where(labels == 1, 0.0, 0.5)).astype(F32)
    by_column = pixel_weight.T
    rows = []
    for r in range(num_rows):
        rows.append((by_column[:, r : r + 1] * cot_ref[r].astype(F32)).astype(BF))
    for r in range(num_rows):
        ig_ref[r] = rows[r]
    edge[last] = ig_ref[edge_row]
    pl.semaphore_wait(barrier, len(peers))
    halo_copy(last).start()
    zero_row = jnp.zeros((num_cols, 3 * channels), BF)
    for buf in range(2):
        taps[buf, 0] = zero_row
        taps[buf, num_rows + 1] = zero_row
    build_taps(last % 2, ig_ref[...].reshape(pixels, channels))

    def core_copy(l):
        return remote(sent.at[l, 1 - core], r1.at[l], s1.at[l], t1.at[l], core_peer())

    def plane_copy(l, j):
        return remote(
            half.at[l, plane_quarter(j)], r2.at[l, j - 1], s2.at[l, j - 1], t2.at[l, j - 1],
            plane_peer(j),
        )

    def depth_copy(l, j):
        return remote(
            quart.at[l, lax.min(depth_index(j), reducers - 1)], r3.at[l, j - 1],
            s3.at[l, j - 1], t3.at[l, j - 1], depth_peer(j),
        )

    def chunk_at(depth):
        return (core * 4 + quarter) * reducers + lax.min(depth, reducers - 1)

    def depth_back(l, j, place):
        return remote(full.at[l, place], full.at[l, place], s4.at[l, j - 1], t4.at[l, j - 1],
                      depth_peer(j))

    def plane_back(l, j, from_quarter):
        place = pl.ds((core * 4 + from_quarter) * reducers, reducers)
        return remote(full.at[l, place], full.at[l, place], s5.at[l, j - 1], t5.at[l, j - 1],
                      plane_peer(j))

    def core_back(l, from_core):
        place = pl.ds(from_core * 4 * reducers, 4 * reducers)
        return remote(full.at[l, place], full.at[l, place], s6.at[l], t6.at[l], core_peer())

    def stage_b(l):
        core_copy(l).wait()
        total = sent[l, core].astype(F32) + r1[l].astype(F32)
        half[l] = total.astype(BF).reshape(half.shape[1:])
        for j in range(1, 4):
            plane_copy(l, j).start()

    def stage_c(l):
        for j in range(1, 4):
            plane_copy(l, j).wait()
        total = half[l, quarter].astype(F32)
        for j in range(3):
            total = total + r2[l, j].astype(F32)
        quart[l] = total.astype(BF).reshape(quart.shape[1:])
        for j in range(1, depth_count):
            @pl.when(depth_index(j) < reducers)
            def _():
                depth_copy(l, j).start()

    def stage_d(l):
        for j in range(1, depth_count):
            @pl.when(depth_index(j) < reducers)
            def _():
                depth_copy(l, j).wait_send()

        @pl.when(z < reducers)
        def _():
            for j in range(1, depth_count):
                depth_copy(l, j).wait_recv()
            total = quart[l, lax.min(z, reducers - 1)].astype(F32)
            for j in range(depth_count - 1):
                total = total + r3[l, j].astype(F32)
            full[l, chunk_at(z)] = (total * grad_scale).astype(BF)
            for j in range(1, depth_count):
                depth_back(l, j, chunk_at(z)).start()

    def stage_e(l):
        for j in range(1, depth_count):
            source = depth_index(depth_count - j)

            @pl.when(source < reducers)
            def _():
                depth_back(l, j, chunk_at(source)).wait_recv()

        @pl.when(z < reducers)
        def _():
            for j in range(1, depth_count):
                depth_back(l, j, chunk_at(z)).wait_send()
        for j in range(1, 4):
            plane_back(l, j, quarter).start()

    def stage_f(l):
        for j in range(1, 4):
            plane_back(l, j, plane_quarter(j)).wait_recv()
            plane_back(l, j, quarter).wait_send()
        core_back(l, core).start()

    def stage_h(l):
        core_back(l, 1 - core).wait_recv()
        core_back(l, core).wait_send()
        slot = slots_ref[l]
        grad_half = full[l].reshape(9 * channels, channels)
        left = jnp.dot(a_all[slot], grad_half, preferred_element_type=F32)
        pre_ref[l] = jnp.dot(left.astype(BF), g_all[slot], preferred_element_type=F32)

    def factors_here(l):
        if l == last:
            for copy in factor_copies():
                copy.wait()

    stages = [
        (1.3, stage_b), (5.5, stage_c), (8.8, stage_d), (12.0, stage_e), (16.0, stage_f),
        (17.2, factors_here), (17.2, stage_h),
    ]
    pending = []

    def launch(l, now):
        core_copy(l).start()
        pending.extend((now + delay, -l, place) for place, (delay, _) in enumerate(stages))
        pending.sort(key=lambda event: (event[0], event[1], event[2]))

    def run_until(now):
        while pending and pending[0][0] <= now:
            _, minus_l, place = pending.pop(0)
            stages[place][1](-minus_l)

    contract_last = (((1,), (1,)), ((), ()))
    contract_first = (((0,), (0,)), ((), ()))

    def tap_rows(buf, a):
        return taps[buf, 2 - a : 2 - a + num_rows].reshape(pixels, 3 * channels)

    def bulk_side(l):
        side = jnp.zeros((pixels, channels), F32)
        for a in range(3):
            side += lax.dot_general(
                tap_rows(l % 2, a), wt[l, :, a * 3 * channels : (a + 1) * 3 * channels],
                contract_last, preferred_element_type=F32,
            )
        return side

    def weight_grad(l):
        flat_inputs = x_ref[l].reshape(pixels, channels)
        for a in range(3):
            block = lax.dot_general(
                flat_inputs, tap_rows(l % 2, a), contract_first, preferred_element_type=F32
            )
            for b in range(3):
                grad32[pl.ds(3 * a + b, channels, stride=9), :] = block[
                    :, b * channels : (b + 1) * channels
                ]
        sent[l] = grad32[...].astype(BF).reshape(sent.shape[1:])

    late_copies = factor_copies()
    for l in range(last, -1, -1):
        buf = l % 2
        now = 4.0 * (last - l)
        w_load(l).wait()
        build_weights(l)
        if l == last:
            a_load.wait()
            g_load.wait()
        x_load(l).wait()
        halo_copy(l).wait()
        for b, piece in enumerate(column_shifts(halo[l].astype(F32))):
            taps[buf, halo_row, :, b * channels : (b + 1) * channels] = piece
        if l > 0:
            side = jnp.zeros((num_cols, channels), F32)
            for a in range(3):
                side += lax.dot_general(
                    taps[buf, edge_row + 2 - a],
                    wt[l, :, a * 3 * channels : (a + 1) * 3 * channels],
                    contract_last, preferred_element_type=F32,
                )
            edge[l - 1] = jnp.where(x_ref[l, edge_row].astype(F32) > 0, side, 0.0).astype(BF)
            halo_copy(l - 1).start()
            if late_copies:
                late_copies.pop(0).start()
            run_until(now + 0.8)
            active = x_ref[l].reshape(pixels, channels).astype(F32) > 0
            build_taps(1 - buf, jnp.where(active, bulk_side(l), 0.0).astype(BF))
            run_until(now + 2.2)
            weight_grad(l)
            launch(l, now + 4.0)
            run_until(now + 4.0)
        else:
            for copy in late_copies:
                copy.start()
            run_until(now + 0.8)
            weight_grad(l)
            launch(l, now + 2.6)
            run_until(now + 2.6)
            ig_ref[...] = bulk_side(l).astype(BF).reshape(num_rows, num_cols, channels)
    run_until(float("inf"))


def reducer_count(quarter_rows, depth_count):
    for count in range(depth_count, 0, -1):
        if quarter_rows % (16 * count) == 0:
            return count
    return 0


def fused_per_device(
    layer_inputs, weights, top_cotangent, segmentation, layer_slots, a_inverse, g_inverse
):
    layer_count = layer_inputs.shape[0]
    num_rows, num_cols, channels = layer_inputs.shape[2:]
    taps_rows = 9 * channels
    data_devices = lax.axis_size("dp")
    owner_devices = lax.axis_size("own")
    grad_scale = 1.0 / math.sqrt(data_devices * owner_devices * num_rows * num_cols)
    depth_count = data_devices // 4
    quarter_rows = taps_rows // 8
    reducers = reducer_count(quarter_rows, depth_count)
    chunk = quarter_rows // reducers
    slots_total = a_inverse.shape[0] * owner_devices
    n = layer_count
    vmem = pl.BlockSpec(memory_space=pltpu.VMEM)
    dma = pltpu.SemaphoreType.DMA
    return pl.pallas_call(
        functools.partial(whole_step_kernel, depth_count, reducers, grad_scale),
        out_shape=(
            jax.ShapeDtypeStruct((n, a_inverse.shape[1], channels), F32),
            jax.ShapeDtypeStruct((num_rows, num_cols, channels), BF),
        ),
        in_specs=[pl.BlockSpec(memory_space=pltpu.SMEM)] + [pl.BlockSpec(memory_space=pltpu.HBM)] * 6,
        out_specs=(vmem, vmem),
        scratch_shapes=[
            pltpu.VMEM((2, num_rows + 2, num_cols, 3 * channels), BF),
            pltpu.VMEM((taps_rows, channels), F32),
            pltpu.VMEM((n, channels, taps_rows), BF),
            pltpu.VMEM((taps_rows, channels), F32),
            pltpu.VMEM((n, 2, taps_rows // 2, channels), BF),
            pltpu.VMEM((n, taps_rows // 2, channels), BF),
            pltpu.VMEM((n, 4, quarter_rows, channels), BF),
            pltpu.VMEM((n, 3, quarter_rows, channels), BF),
            pltpu.VMEM((n, reducers, chunk, channels), BF),
            pltpu.VMEM((n, depth_count - 1, chunk, channels), BF),
            pltpu.VMEM((n, 8 * reducers, chunk, channels), BF),
            pltpu.VMEM((n, num_cols, channels), BF),
            pltpu.VMEM((n, num_cols, channels), BF),
            pltpu.VMEM((slots_total,) + a_inverse.shape[1:], BF),
            pltpu.VMEM((slots_total,) + g_inverse.shape[1:], BF),
            pltpu.VMEM((n, num_rows, num_cols, channels), BF),
            pltpu.VMEM((n, taps_rows, channels), BF),
            pltpu.VMEM((num_rows, num_cols, channels), BF),
            pltpu.VMEM((num_rows, num_cols), jnp.int32),
            dma((4 + 2 * n,)),
            dma((n,)), dma((n,)), dma((a_inverse.shape[0] + 1,)), dma((a_inverse.shape[0] + 1,)),
            dma((n,)), dma((n,)), dma((n, 3)), dma((n, 3)),
            dma((n, depth_count - 1)), dma((n, depth_count - 1)),
            dma((n, depth_count - 1)), dma((n, depth_count - 1)),
            dma((n, 3)), dma((n, 3)), dma((n,)), dma((n,)),
        ],
        compiler_params=pltpu.CompilerParams(
            collective_id=0, has_side_effects=True, vmem_limit_bytes=48 * 1024 * 1024
        ),
        name="whole_step",
    )(
        layer_slots, layer_inputs[:, 0], weights, top_cotangent[0], segmentation[0],
        a_inverse, g_inverse,
    )


def fused_step(*args):
    preconditioned, input_grad = fused_per_device(*args)
    return (preconditioned, input_grad[None])


def solution(mesh):
    in_specs = (
        P(None, "dp", "own", None, None),
        P(),
        P("dp", "own", None, None),
        P("dp", "own", None),
        P(),
        P("own", "dp", None),
        P("own", None, None),
    )
    out_specs = (P(None, "dp", None), P("dp", "own", None, None))
    fits = mesh.shape["own"] == 2 and mesh.shape["dp"] == 16
    return jax.shard_map(
        fused_step if fits else per_device,
        mesh=mesh, in_specs=in_specs, out_specs=out_specs, check_vma=False,
    )
```

```python
import functools
import math

import jax
import jax.numpy as jnp
from jax import lax
from jax.experimental import pallas as pl
from jax.experimental.pallas import tpu as pltpu
from jax.sharding import PartitionSpec as P


def extended(cells, sides, width):
    for axis, dim in sides:
        count = lax.axis_size(axis)
        ends = count - 1
        head = lax.slice_in_dim(cells, 0, width, axis=dim)
        tail = lax.slice_in_dim(cells, cells.shape[dim] - width, cells.shape[dim], axis=dim)
        cells = jnp.concatenate(
            [
                lax.ppermute(tail, axis, [(i, (i + 1) % count) for i in range(ends)]),
                cells,
                lax.ppermute(head, axis, [((i + 1) % count, i) for i in range(ends)]),
            ],
            axis=dim,
        )
    return cells


def from_root(block, axis, owner):
    block = jnp.where(lax.axis_index(axis) == owner, block, jnp.zeros_like(block))
    return lax.psum(block, axis)


def loss_weight(labels):
    return jnp.where(labels == 0, 1.0, jnp.where(labels == 1, 0.0, 0.5)).astype(jnp.float32)


def tap_matrix(padded, num_rows, num_cols):
    channels = padded.shape[-1]
    pieces = []
    for tap_index in range(9):
        row_start = 2 - tap_index // 3
        col_start = 2 - tap_index % 3
        pieces.append(padded[row_start : row_start + num_rows, col_start : col_start + num_cols])
    stacked = jnp.stack(pieces, axis=2)
    return stacked.reshape(num_rows * num_cols, 9 * channels)


def per_device(
    layer_inputs, weights, top_cotangent, segmentation, layer_slots, a_inverse, g_inverse
):
    layer_count = layer_inputs.shape[0]
    num_rows = layer_inputs.shape[2]
    num_cols = layer_inputs.shape[3]
    channels = layer_inputs.shape[4]
    data_devices = lax.axis_size("dp")
    owner_devices = lax.axis_size("own")
    grad_scale = 1.0 / math.sqrt(data_devices * owner_devices * num_rows * num_cols)
    inputs_local = layer_inputs[:, 0]
    scaled = loss_weight(segmentation[0])[:, :, None] * top_cotangent[0].astype(jnp.float32)
    out_grad = scaled.astype(jnp.bfloat16)
    grad_blocks = [None] * layer_count
    input_grad = None
    for layer_index in range(layer_count - 1, -1, -1):
        rimmed = extended(out_grad, (("own", 0),), 1)
        padded = jnp.pad(rimmed, ((0, 0), (1, 1), (0, 0)))
        tap_rows = tap_matrix(padded, num_rows, num_cols)
        flat_inputs = inputs_local[layer_index].reshape(num_rows * num_cols, channels)
        grad_block = lax.dot_general(
            flat_inputs, tap_rows, (((0,), (0,)), ((), ())), preferred_element_type=jnp.float32
        )
        grad_blocks[layer_index] = grad_block.reshape(9 * channels, channels) * grad_scale
        kernel = weights[layer_index].reshape(channels, 9 * channels)
        input_side = lax.dot_general(
            tap_rows, kernel, (((1,), (1,)), ((), ())), preferred_element_type=jnp.float32
        )
        input_side = input_side.reshape(num_rows, num_cols, channels)
        if layer_index > 0:
            out_grad = jnp.where(inputs_local[layer_index] > 0, input_side, 0.0).astype(
                jnp.bfloat16
            )
        else:
            input_grad = input_side.astype(jnp.bfloat16)[None]
    grad_term = jnp.concatenate(grad_blocks, axis=1)
    grad_rows = lax.psum_scatter(grad_term, "dp", scatter_dimension=0, tiled=True)
    slot_count = a_inverse.shape[0]
    grad_sum = lax.psum(grad_rows.astype(jnp.bfloat16), "own")
    left_panels = []
    right_panels = []
    for layer_index in range(layer_count):
        slot_id = layer_slots[layer_index]
        owner_index = slot_id // slot_count
        local_slot = slot_id % slot_count
        left_panel = lax.dynamic_index_in_dim(a_inverse, local_slot, 0, keepdims=False)
        right_panel = lax.dynamic_index_in_dim(g_inverse, local_slot, 0, keepdims=False)
        left_panel, right_panel = (
            from_root(left_panel, "own", owner_index),
            from_root(right_panel, "own", owner_index),
        )
        left_panels.append(left_panel)
        right_panels.append(right_panel)
    left_stack = jnp.stack(left_panels, axis=0)
    right_stack = jnp.stack(right_panels, axis=0)
    gathered_piece = lax.all_gather(grad_sum, "dp", axis=0, tiled=True)
    width_here = gathered_piece.shape[0]
    shaped_piece = gathered_piece.reshape(width_here, layer_count, channels)
    left_product = jnp.einsum(
        "lrn,nlc->lrc", left_stack, shaped_piece, preferred_element_type=jnp.float32
    )
    preconditioned = jnp.einsum(
        "lrc,lcd->lrd",
        left_product.astype(jnp.bfloat16),
        right_stack,
        preferred_element_type=jnp.float32,
    )
    return (preconditioned, input_grad)


BF = jnp.bfloat16
F32 = jnp.float32
MESH = pl.DeviceIdType.MESH


def whole_step_kernel(
    depth_count, reducers, grad_scale,
    slots_ref, x_hbm, w_hbm, cot_hbm, seg_hbm, a_hbm, gi_hbm,
    pre_ref, ig_ref,
    taps, w32, wt, grad32, sent, r1, half, r2, quart, r3, full,
    edge, halo, a_all, g_all, x_ref, w_ref, cot_ref, seg_ref, load,
    halo_s, halo_r, ex_s, ex_r, s1, t1, s2, t2, s3, t3, s4, t4, s5, t5, s6, t6,
):
    layer_count, num_rows, num_cols, channels = x_ref.shape
    pixels = num_rows * num_cols
    dp = lax.axis_index("dp")
    own = lax.axis_index("own")
    core = lax.rem(dp, 2)
    y = lax.rem(dp // 2, 2)
    z = dp // 4
    quarter = y * 2 + own
    slot_count = a_hbm.shape[0]
    held = pl.ds(own * slot_count, slot_count)

    def core_peer():
        return (dp + 1 - 2 * core, own)

    def plane_peer(j):
        other_y = y if j < 2 else 1 - y
        other_own = own if j % 2 == 0 else 1 - own
        return ((z * 2 + other_y) * 2 + core, other_own)

    def plane_quarter(j):
        other_y = y if j < 2 else 1 - y
        other_own = own if j % 2 == 0 else 1 - own
        return other_y * 2 + other_own

    def depth_index(j):
        return lax.rem(z + j, depth_count)

    def depth_peer(j):
        return ((depth_index(j) * 2 + y) * 2 + core, own)

    def remote(src, dst, send_sem, recv_sem, device):
        return pltpu.make_async_remote_copy(
            src_ref=src, dst_ref=dst, send_sem=send_sem, recv_sem=recv_sem,
            device_id=device, device_id_type=MESH,
        )

    last = layer_count - 1
    cot_load = pltpu.make_async_copy(cot_hbm, cot_ref, load.at[0])
    seg_load = pltpu.make_async_copy(seg_hbm, seg_ref, load.at[1])
    a_load = pltpu.make_async_copy(a_hbm, a_all.at[held], load.at[2])
    g_load = pltpu.make_async_copy(gi_hbm, g_all.at[held], load.at[3])

    def x_load(l):
        return pltpu.make_async_copy(x_hbm.at[l], x_ref.at[l], load.at[4 + l])

    def w_load(l):
        return pltpu.make_async_copy(w_hbm.at[l], w_ref.at[l], load.at[4 + layer_count + l])

    seg_load.start()
    cot_load.start()
    w_load(last).start()
    x_load(last).start()
    a_load.start()
    g_load.start()
    for l in range(last - 1, -1, -1):
        w_load(l).start()
        x_load(l).start()

    barrier = pltpu.get_barrier_semaphore()
    peers = [core_peer()] + [plane_peer(j) for j in range(1, 4)]
    peers += [depth_peer(j) for j in range(1, depth_count)]
    for peer in peers:
        pl.semaphore_signal(barrier, inc=1, device_id=peer, device_id_type=MESH)

    col_index = lax.broadcasted_iota(jnp.int32, (pixels, channels), 0) % num_cols

    def column_shifts(flat):
        count = flat.shape[0]
        index = col_index[:count]
        before = jnp.where(index == num_cols - 1, 0.0, pltpu.roll(flat, count - 1, 0))
        after = jnp.where(index == 0, 0.0, pltpu.roll(flat, 1, 0))
        return (before.astype(BF), flat.astype(BF), after.astype(BF))

    def build_taps(buf, grad):
        flat = grad.astype(F32)
        for b, piece in enumerate(column_shifts(flat)):
            taps[buf, 1 : num_rows + 1, :, b * channels : (b + 1) * channels] = piece.reshape(
                num_rows, num_cols, channels
            )

    halo_row = (num_rows + 1) * (1 - own)
    edge_row = (num_rows - 1) * (1 - own)

    def halo_copy(l):
        return remote(edge.at[l], halo.at[l], halo_s.at[l], halo_r.at[l], (dp, 1 - own))

    def a_copy(k):
        place = a_all.at[own * slot_count + k]
        return remote(place, place, ex_s.at[k], ex_r.at[k], (dp, 1 - own))

    def g_copy():
        return remote(g_all.at[held], g_all.at[held], ex_s.at[slot_count], ex_r.at[slot_count],
                      (dp, 1 - own))

    def factor_copies():
        return [a_copy(k) for k in range(slot_count)] + [g_copy()]

    def build_weights(l):
        w32[...] = w_ref[l].astype(F32)
        for k in range(9):
            wt[l, :, k * channels : (k + 1) * channels] = w32[
                pl.ds(k, channels, stride=9), :
            ].astype(BF)

    seg_load.wait()
    cot_load.wait()
    labels = seg_ref[...]
    pixel_weight = jnp.where(labels == 0, 1.0, jnp.where(labels == 1, 0.0, 0.5)).astype(F32)
    by_column = pixel_weight.T
    rows = []
    for r in range(num_rows):
        rows.append((by_column[:, r : r + 1] * cot_ref[r].astype(F32)).astype(BF))
    for r in range(num_rows):
        ig_ref[r] = rows[r]
    edge[last] = ig_ref[edge_row]
    pl.semaphore_wait(barrier, len(peers))
    halo_copy(last).start()
    zero_row = jnp.zeros((num_cols, 3 * channels), BF)
    for buf in range(2):
        taps[buf, 0] = zero_row
        taps[buf, num_rows + 1] = zero_row
    build_taps(last % 2, ig_ref[...].reshape(pixels, channels))

    def core_copy(l):
        return remote(sent.at[l, 1 - core], r1.at[l], s1.at[l], t1.at[l], core_peer())

    def plane_copy(l, j):
        return remote(
            half.at[l, plane_quarter(j)], r2.at[l, j - 1], s2.at[l, j - 1], t2.at[l, j - 1],
            plane_peer(j),
        )

    def depth_copy(l, j):
        return remote(
            quart.at[l, lax.min(depth_index(j), reducers - 1)], r3.at[l, j - 1],
            s3.at[l, j - 1], t3.at[l, j - 1], depth_peer(j),
        )

    def chunk_at(depth):
        return (core * 4 + quarter) * reducers + lax.min(depth, reducers - 1)

    def depth_back(l, j, place):
        return remote(full.at[l, place], full.at[l, place], s4.at[l, j - 1], t4.at[l, j - 1],
                      depth_peer(j))

    def plane_back(l, j, from_quarter):
        place = pl.ds((core * 4 + from_quarter) * reducers, reducers)
        return remote(full.at[l, place], full.at[l, place], s5.at[l, j - 1], t5.at[l, j - 1],
                      plane_peer(j))

    def core_back(l, from_core):
        place = pl.ds(from_core * 4 * reducers, 4 * reducers)
        return remote(full.at[l, place], full.at[l, place], s6.at[l], t6.at[l], core_peer())

    def stage_b(l):
        core_copy(l).wait()
        total = sent[l, core].astype(F32) + r1[l].astype(F32)
        half[l] = total.astype(BF).reshape(half.shape[1:])
        for j in range(1, 4):
            plane_copy(l, j).start()

    def stage_c(l):
        for j in range(1, 4):
            plane_copy(l, j).wait()
        total = half[l, quarter].astype(F32)
        for j in range(3):
            total = total + r2[l, j].astype(F32)
        quart[l] = total.astype(BF).reshape(quart.shape[1:])
        for j in range(1, depth_count):
            @pl.when(depth_index(j) < reducers)
            def _():
                depth_copy(l, j).start()

    def stage_d(l):
        for j in range(1, depth_count):
            @pl.when(depth_index(j) < reducers)
            def _():
                depth_copy(l, j).wait_send()

        @pl.when(z < reducers)
        def _():
            for j in range(1, depth_count):
                depth_copy(l, j).wait_recv()
            total = quart[l, lax.min(z, reducers - 1)].astype(F32)
            for j in range(depth_count - 1):
                total = total + r3[l, j].astype(F32)
            full[l, chunk_at(z)] = (total * grad_scale).astype(BF)
            for j in range(1, depth_count):
                depth_back(l, j, chunk_at(z)).start()

    def stage_e(l):
        for j in range(1, depth_count):
            source = depth_index(depth_count - j)

            @pl.when(source < reducers)
            def _():
                depth_back(l, j, chunk_at(source)).wait_recv()

        @pl.when(z < reducers)
        def _():
            for j in range(1, depth_count):
                depth_back(l, j, chunk_at(z)).wait_send()
        for j in range(1, 4):
            plane_back(l, j, quarter).start()

    def stage_f(l):
        for j in range(1, 4):
            plane_back(l, j, plane_quarter(j)).wait_recv()
            plane_back(l, j, quarter).wait_send()
        core_back(l, core).start()

    def stage_h(l):
        core_back(l, 1 - core).wait_recv()
        core_back(l, core).wait_send()
        slot = slots_ref[l]
        grad_half = full[l].reshape(9 * channels, channels)
        left = jnp.dot(a_all[slot], grad_half, preferred_element_type=F32)
        pre_ref[l] = jnp.dot(left.astype(BF), g_all[slot], preferred_element_type=F32)

    def factors_here(l):
        if l == last:
            for copy in factor_copies():
                copy.wait()

    stages = [
        (1.3, stage_b), (5.5, stage_c), (8.8, stage_d), (12.0, stage_e), (16.0, stage_f),
        (17.2, factors_here), (17.2, stage_h),
    ]
    pending = []

    def launch(l, now):
        core_copy(l).start()
        pending.extend((now + delay, -l, place) for place, (delay, _) in enumerate(stages))
        pending.sort(key=lambda event: (event[0], event[1], event[2]))

    def run_until(now):
        while pending and pending[0][0] <= now:
            _, minus_l, place = pending.pop(0)
            stages[place][1](-minus_l)

    contract_last = (((1,), (1,)), ((), ()))
    contract_first = (((0,), (0,)), ((), ()))

    def tap_rows(buf, a):
        return taps[buf, 2 - a : 2 - a + num_rows].reshape(pixels, 3 * channels)

    def bulk_side(l):
        side = jnp.zeros((pixels, channels), F32)
        for a in range(3):
            side += lax.dot_general(
                tap_rows(l % 2, a), wt[l, :, a * 3 * channels : (a + 1) * 3 * channels],
                contract_last, preferred_element_type=F32,
            )
        return side

    def weight_grad(l):
        flat_inputs = x_ref[l].reshape(pixels, channels)
        for a in range(3):
            block = lax.dot_general(
                flat_inputs, tap_rows(l % 2, a), contract_first, preferred_element_type=F32
            )
            for b in range(3):
                grad32[pl.ds(3 * a + b, channels, stride=9), :] = block[
                    :, b * channels : (b + 1) * channels
                ]
        sent[l] = grad32[...].astype(BF).reshape(sent.shape[1:])

    late_copies = factor_copies()
    for l in range(last, -1, -1):
        buf = l % 2
        now = 4.0 * (last - l)
        w_load(l).wait()
        build_weights(l)
        if l == last:
            a_load.wait()
            g_load.wait()
        x_load(l).wait()
        halo_copy(l).wait()
        for b, piece in enumerate(column_shifts(halo[l].astype(F32))):
            taps[buf, halo_row, :, b * channels : (b + 1) * channels] = piece
        if l > 0:
            side = jnp.zeros((num_cols, channels), F32)
            for a in range(3):
                side += lax.dot_general(
                    taps[buf, edge_row + 2 - a],
                    wt[l, :, a * 3 * channels : (a + 1) * 3 * channels],
                    contract_last, preferred_element_type=F32,
                )
            edge[l - 1] = jnp.where(x_ref[l, edge_row].astype(F32) > 0, side, 0.0).astype(BF)
            halo_copy(l - 1).start()
            if late_copies:
                late_copies.pop(0).start()
            run_until(now + 0.8)
            active = x_ref[l].reshape(pixels, channels).astype(F32) > 0
            build_taps(1 - buf, jnp.where(active, bulk_side(l), 0.0).astype(BF))
            run_until(now + 2.2)
            weight_grad(l)
            launch(l, now + 4.0)
            run_until(now + 4.0)
        else:
            for copy in late_copies:
                copy.start()
            run_until(now + 0.8)
            weight_grad(l)
            launch(l, now + 2.6)
            run_until(now + 2.6)
            ig_ref[...] = bulk_side(l).astype(BF).reshape(num_rows, num_cols, channels)
    run_until(float("inf"))


def reducer_count(quarter_rows, depth_count):
    for count in range(depth_count, 0, -1):
        if quarter_rows % (16 * count) == 0:
            return count
    return 0


def fused_per_device(
    layer_inputs, weights, top_cotangent, segmentation, layer_slots, a_inverse, g_inverse
):
    layer_count = layer_inputs.shape[0]
    num_rows, num_cols, channels = layer_inputs.shape[2:]
    taps_rows = 9 * channels
    data_devices = lax.axis_size("dp")
    owner_devices = lax.axis_size("own")
    grad_scale = 1.0 / math.sqrt(data_devices * owner_devices * num_rows * num_cols)
    depth_count = data_devices // 4
    quarter_rows = taps_rows // 8
    reducers = reducer_count(quarter_rows, depth_count)
    chunk = quarter_rows // reducers
    slots_total = a_inverse.shape[0] * owner_devices
    n = layer_count
    vmem = pl.BlockSpec(memory_space=pltpu.VMEM)
    dma = pltpu.SemaphoreType.DMA
    return pl.pallas_call(
        functools.partial(whole_step_kernel, depth_count, reducers, grad_scale),
        out_shape=(
            jax.ShapeDtypeStruct((n, a_inverse.shape[1], channels), F32),
            jax.ShapeDtypeStruct((num_rows, num_cols, channels), BF),
        ),
        in_specs=[pl.BlockSpec(memory_space=pltpu.SMEM)] + [pl.BlockSpec(memory_space=pltpu.HBM)] * 6,
        out_specs=(vmem, vmem),
        scratch_shapes=[
            pltpu.VMEM((2, num_rows + 2, num_cols, 3 * channels), BF),
            pltpu.VMEM((taps_rows, channels), F32),
            pltpu.VMEM((n, channels, taps_rows), BF),
            pltpu.VMEM((taps_rows, channels), F32),
            pltpu.VMEM((n, 2, taps_rows // 2, channels), BF),
            pltpu.VMEM((n, taps_rows // 2, channels), BF),
            pltpu.VMEM((n, 4, quarter_rows, channels), BF),
            pltpu.VMEM((n, 3, quarter_rows, channels), BF),
            pltpu.VMEM((n, reducers, chunk, channels), BF),
            pltpu.VMEM((n, depth_count - 1, chunk, channels), BF),
            pltpu.VMEM((n, 8 * reducers, chunk, channels), BF),
            pltpu.VMEM((n, num_cols, channels), BF),
            pltpu.VMEM((n, num_cols, channels), BF),
            pltpu.VMEM((slots_total,) + a_inverse.shape[1:], BF),
            pltpu.VMEM((slots_total,) + g_inverse.shape[1:], BF),
            pltpu.VMEM((n, num_rows, num_cols, channels), BF),
            pltpu.VMEM((n, taps_rows, channels), BF),
            pltpu.VMEM((num_rows, num_cols, channels), BF),
            pltpu.VMEM((num_rows, num_cols), jnp.int32),
            dma((4 + 2 * n,)),
            dma((n,)), dma((n,)), dma((a_inverse.shape[0] + 1,)), dma((a_inverse.shape[0] + 1,)),
            dma((n,)), dma((n,)), dma((n, 3)), dma((n, 3)),
            dma((n, depth_count - 1)), dma((n, depth_count - 1)),
            dma((n, depth_count - 1)), dma((n, depth_count - 1)),
            dma((n, 3)), dma((n, 3)), dma((n,)), dma((n,)),
        ],
        compiler_params=pltpu.CompilerParams(
            collective_id=0, has_side_effects=True, vmem_limit_bytes=60 * 1024 * 1024
        ),
        name="whole_step",
    )(
        layer_slots, layer_inputs[:, 0], weights, top_cotangent[0], segmentation[0],
        a_inverse, g_inverse,
    )


def fused_step(*args):
    preconditioned, input_grad = fused_per_device(*args)
    return (preconditioned, input_grad[None])


def solution(mesh):
    in_specs = (
        P(None, "dp", "own", None, None),
        P(),
        P("dp", "own", None, None),
        P("dp", "own", None),
        P(),
        P("own", "dp", None),
        P("own", None, None),
    )
    out_specs = (P(None, "dp", None), P("dp", "own", None, None))
    fits = mesh.shape["own"] == 2 and mesh.shape["dp"] == 16
    return jax.shard_map(
        fused_step if fits else per_device,
        mesh=mesh, in_specs=in_specs, out_specs=out_specs, check_vma=False,
    )
```
